32 devices in a mesh: grp: 4 (over z), dev: 8 (over y, x, core).
Axes of the slice: x: 2, y: 2, z: 4, core: 2. Of those that a mesh axis runs over, the one named last changes fastest.
Arguments:
- inv_factor: bfloat16 [128, 384, 384], P(('grp', 'dev')), may hold values from -8 to 8
- border: bfloat16 [128, 384, 2048], P(('grp', 'dev')), may hold values from -0.107910156 to 0.107910156
- block_rows: int32 [128], P(('grp', 'dev')), may hold values from 96 to 384
- live_count: int32 [32], P(('grp', 'dev')), may hold values from 1 to 4, as said below
- first_section: float32 [2048, 2048], P('dev'), may hold values from -6 to 6
Outputs:
- condensed: bfloat16 [128, 384, 2048], P(('grp', 'dev'))
- schur: float32 [2048, 2048], P('dev')
The draws below stay inside these ranges and needn't reach their ends.
Inputs may be any that keep to these rules, and one draw needn't show every extreme that they name: `live_count`: every device holds 1 to 4 live scenarios; at least one device holds 4.
All inputs are finite; a program needn't handle non-finite values.
Results may differ from the reference program's by a relative error of at most 0.001.
Values sent between devices are 32-bit elements; how exact they have to be, the bound alone decides.
No kernel may reach another device: no remote copies, remote signals or barrier semaphores. Data moves between devices by JAX's collectives and lax.ppermute only.
A program may use at most 192 MiB of HBM per device.

```python
import jax
import jax.numpy as jnp
from jax import lax

NB = 384
NS = 2048
SLOT = 4
SCEN = 128
DEVICES = 32


def draw_inv_factor(key, part):
    key_off = jax.random.fold_in(key, 11)
    key_diag = jax.random.fold_in(key, 12)
    offdiag = jax.random.normal(key_off, (SCEN, NB, NB), jnp.float32) * (0.3 / NB ** 0.5)
    offdiag = jnp.clip(offdiag, -0.1, 0.1)
    diag_vals = jax.random.uniform(key_diag, (SCEN, NB), jnp.float32, 1.0, 1.9)
    matrix = offdiag + jnp.eye(NB, dtype=jnp.float32)[None] * diag_vals[:, :, None]
    return matrix.astype(jnp.bfloat16)


def draw_live_count(key, part):
    key_one = jax.random.fold_in(key, 21)
    key_two = jax.random.fold_in(key, 22)
    key_pick = jax.random.fold_in(key, 23)
    first_draw = jax.random.randint(key_one, (DEVICES,), 1, SLOT + 1)
    second_draw = jax.random.randint(key_two, (DEVICES,), 1, SLOT + 1)
    values = jnp.minimum(first_draw, second_draw)
    chosen = jax.random.randint(key_pick, (), 0, DEVICES)
    values = jnp.where(jnp.arange(DEVICES) == chosen, SLOT, values)
    return values.astype(jnp.int32)


def with_ends(array, own_key, smallest, top_value):
    longest = array.shape.index(max(array.shape))
    spots = []
    for shift in (0, 1):
        where = [jax.random.randint(jax.random.fold_in(own_key, axis), (), 0, length) for axis, length in enumerate(array.shape)]
        where[longest] = (where[longest] + shift) % array.shape[longest]
        spots.append(tuple(where))
    return array.at[spots[0]].set(smallest).at[spots[1]].set(top_value)


def block_scale(key, shape, cuts, least, top_value):
    level = 1.0
    for axis_at, parts in cuts:
        steps = jax.random.uniform(jax.random.fold_in(jax.random.fold_in(key, 6), axis_at), (parts,), jnp.float32, least / len(cuts), top_value / len(cuts))
        level = level * jnp.repeat(jnp.exp(steps), shape[axis_at] // parts).reshape((-1,) + (1,) * (len(shape) - 1 - axis_at))
    return level


def bell_draw(rng, extent, width, bound, pieces=(), kind=jnp.bfloat16):
    array = jax.random.normal(rng, extent, jnp.float32) * width
    if len(pieces) > 0:
        array = block_scale(rng, extent, pieces, -0.22, 0.18) * array
    return jnp.clip(array, min=-bound, max=bound).astype(kind)


def setup_inputs(seed: int = 0) -> dict:
    keys = jax.random.split(jax.random.key(seed), 6)
    inv_factor = draw_inv_factor(jax.random.fold_in(keys[5], 71), 0)
    border = bell_draw(keys[1], (SCEN, NB, NS), 0.018, 0.107910156, ((0, 32),))
    block_rows = with_ends(jax.random.randint(keys[2], (SCEN,), NB // 4, NB + 1), jax.random.fold_in(keys[2], 1), NB // 4, NB).astype(jnp.int32)
    live_count = draw_live_count(jax.random.fold_in(keys[5], 71), 0)
    first_section = bell_draw(keys[4], (NS, NS), 1.0, 6.0, ((0, 8),), jnp.float32)
    return {"inv_factor": inv_factor, "border": border, "block_rows": block_rows, "live_count": live_count, "first_section": first_section}


def reference(inv_factor, border, block_rows, live_count, first_section):
    owners = jnp.arange(SCEN, dtype=jnp.int32) // SLOT
    within = jnp.arange(SCEN, dtype=jnp.int32) % SLOT
    alive = within < live_count[owners]
    row_ids = jnp.arange(NB, dtype=jnp.int32)

    def one_slot(running, items):
        inverse, border_piece, rows_live, is_live = items
        keep = (row_ids < rows_live) & is_live
        masked = jnp.where(keep[:, None], inverse, jnp.zeros_like(inverse))

        def compute(running_in):
            product = jnp.dot(masked.astype(jnp.float32), border_piece.astype(jnp.float32),
                              precision=lax.Precision.HIGHEST).astype(jnp.bfloat16)
            wide = product.astype(jnp.float32)
            update = jnp.dot(wide.T, wide, precision=lax.Precision.HIGHEST)
            return running_in + update, product

        def skipped(running_in):
            return running_in, jnp.zeros((NB, NS), jnp.bfloat16)

        return lax.cond(is_live, compute, skipped, running)

    total, condensed = lax.scan(one_slot, jnp.zeros((NS, NS), jnp.float32),
                                (inv_factor, border, block_rows, alive))
    return condensed, first_section - total
```

```python
import functools

import jax
import jax.numpy as jnp
from jax import lax
from jax.experimental import pallas as pl
from jax.experimental.pallas import tpu as pltpu
from jax.sharding import PartitionSpec as P


F32 = jnp.float32
ANY = pl.ANY


def power_of_two(n):
    return n >= 2 and n & (n - 1) == 0


def plain_body(inv_factor, border, block_rows, live_count, first_section):
    slots, rows_block, _ = border.shape
    row_ids = lax.broadcasted_iota(jnp.int32, (slots, rows_block, 1), 1)
    slot_ids = lax.broadcasted_iota(jnp.int32, (slots, rows_block, 1), 0)
    keep = (row_ids < block_rows[:, None, None]) & (slot_ids < live_count[0])
    masked = jnp.where(keep, inv_factor, jnp.zeros_like(inv_factor))
    condensed = jnp.einsum(
        "srk,skc->src", masked, border, preferred_element_type=F32
    ).astype(border.dtype)
    flat = condensed.reshape(slots * rows_block, -1)
    partial = lax.dot_general(
        flat, flat, (((0,), (0,)), ((), ())), preferred_element_type=F32
    )
    share = lax.psum_scatter(partial, "dev", scatter_dimension=0, tiled=True)
    return condensed, first_section - lax.psum(share, "grp")


def high_of(e, mu):
    chip = e >> 1
    return ((chip ^ mu) < chip).astype(jnp.int32)


def owned_column(e, mu):
    return e ^ (2 * mu + high_of(e, mu))


def received_column(e, mu):
    return e ^ (2 * mu + 1 - high_of(e, mu))


def condense_kernel(info, rows, inv_ref, border_ref, out_ref, turned_ref):
    slot = pl.program_id(0)
    live = slot < info[2]

    @pl.when(live)
    def _():
        inv = inv_ref[0]
        row_ids = lax.broadcasted_iota(jnp.int32, inv.shape, 0)
        inv = jnp.where(row_ids < rows[slot], inv, jnp.zeros_like(inv))
        product = jnp.dot(inv, border_ref[0], preferred_element_type=F32)
        product = product.astype(out_ref.dtype)
        out_ref[0] = product
        turned_ref[...] = product.T

    @pl.when(jnp.logical_not(live))
    def _():
        out_ref[...] = jnp.zeros_like(out_ref)
        turned_ref[...] = jnp.zeros_like(turned_ref)


def condense(info, block_rows, inv_factor, border, tile=512):
    slots, rows, width = border.shape
    tile = min(tile, width)
    last = width // tile - 1

    def source(s, n, info, rows):
        live = s < info[2]
        return (
            jnp.minimum(s, info[2] - 1),
            0,
            jnp.where(live, n, last),
        )

    return pl.pallas_call(
        condense_kernel,
        out_shape=(
            jax.ShapeDtypeStruct(border.shape, border.dtype),
            jax.ShapeDtypeStruct((width, slots * rows), border.dtype),
        ),
        grid_spec=pltpu.PrefetchScalarGridSpec(
            num_scalar_prefetch=2,
            grid=(slots, width // tile),
            in_specs=[
                pl.BlockSpec(
                    (1, rows, rows),
                    lambda s, n, info, rows_: (jnp.minimum(s, info[2] - 1), 0, 0),
                ),
                pl.BlockSpec((1, rows, tile), source),
            ],
            out_specs=(
                pl.BlockSpec((1, rows, tile), lambda s, n, info, rows_: (s, 0, n)),
                pl.BlockSpec((tile, rows), lambda s, n, info, rows_: (n, s)),
            ),
        ),
        cost_estimate=pl.CostEstimate(
            flops=2 * slots * rows * rows * width,
            bytes_accessed=3 * border.size * 2,
            transcendentals=0,
        ),
        name="condense",
    )(info, block_rows, inv_factor, border)


def product_kernel(order, rest, info, *refs):
    *sources, keep_ref, send_ref = refs
    flip = info[1]
    keeps = pl.program_id(0)
    z_at = order.index("z")
    pieces = [jnp.dot(sources[0][...], sources[1][...], preferred_element_type=F32)]
    if rest:
        pieces.append(
            jnp.dot(sources[2][...], sources[3][...], preferred_element_type=F32)
        )

    def store(ref):
        for j in range(2):
            at = 0
            for piece in pieces:
                half = piece.shape[0] // 2
                where = [0] * len(order)
                where[z_at] = j ^ flip
                ref[(*where, pl.ds(at, half), slice(None))] = piece[
                    j * half : (j + 1) * half
                ]
                at += half

    @pl.when(keeps == 0)
    def _():
        store(send_ref)

    @pl.when(keeps == 1)
    def _():
        store(keep_ref)


def products(info, condensed, turned, block, mu, order):
    depth, width = condensed.shape
    rest = mu == 0
    bits = [b for b in order if b != "z"]
    grid = (2,) * (1 + len(bits))

    def owner(ids, info):
        r = 1 - ids[0]
        for one, bit in zip(ids[1:], bits):
            r = r | (one << bit)
        return info[0] ^ r

    n = len(grid)

    def left(*a):
        return owner(a[:n], a[n]), 0

    def right(*a):
        e = owner(a[:n], a[n])
        return 0, (e if rest else owned_column(e, mu))

    def left_shared(*a):
        e = owner(a[:n], a[n])
        return 2 * (e & ~1) + (e & 1), 0

    def right_shared(*a):
        return 0, owner(a[:n], a[n]) | 1

    in_specs = [
        pl.BlockSpec((block, depth), left),
        pl.BlockSpec((depth, block), right),
    ]
    operands = [turned, condensed]
    height = block // 2
    if rest:
        in_specs += [
            pl.BlockSpec((block // 2, depth), left_shared),
            pl.BlockSpec((depth, block), right_shared),
        ]
        operands += [turned, condensed]
        height += block // 4
    shape = (2,) * len(order) + (height, block)
    block_shape = tuple(2 if b == "z" else 1 for b in order) + (height, block)

    def place(ids):
        at = dict(zip(bits, ids))
        return tuple(0 if b == "z" else at[b] for b in order) + (0, 0)

    def keep_map(*a):
        return place([jnp.where(a[0] == 1, i, 0) for i in a[1:n]])

    def send_map(*a):
        return place([jnp.where(a[0] == 0, i, 1) for i in a[1:n]])

    out = jax.ShapeDtypeStruct(shape, F32)
    owners = 2 ** len(grid)
    return pl.pallas_call(
        functools.partial(product_kernel, order, rest),
        out_shape=(out, out),
        grid_spec=pltpu.PrefetchScalarGridSpec(
            num_scalar_prefetch=1,
            grid=grid,
            in_specs=in_specs,
            out_specs=(
                pl.BlockSpec(block_shape, keep_map),
                pl.BlockSpec(block_shape, send_map),
            ),
        ),
        cost_estimate=pl.CostEstimate(
            flops=2 * owners * 2 * height * block * depth,
            bytes_accessed=owners * block * depth * 4 + owners * height * block * 8,
            transcendentals=0,
        ),
        name=f"products_{mu}",
    )(info, *operands)


def swap(x, axis, bits):
    n = lax.axis_size(axis)
    return lax.ppermute(x, axis, [(i, i ^ bits) for i in range(n)])


def reduce_wave(kept, sent, order):
    got = swap(sent, "dev", 1)
    for step in order:
        send = kept[1] + got[1]
        kept = kept[0] + got[0]
        got = swap(send, "grp", 1) if step == "z" else swap(send, "dev", 1 << step)
    mine = kept + got
    bit = 2
    while bit < lax.axis_size("grp"):
        mine = mine + swap(mine, "grp", bit)
        bit *= 2
    return mine, swap(mine, "grp", 1)


def ordered(flip, first, second):
    return jnp.where(flip == 0, first, second), jnp.where(flip == 0, second, first)


def finish_kernel(mu, chained, info, first_ref, *refs):
    refs = refs[1:] if chained else refs
    *parts, out_ref = refs
    me, flip = info[0], info[1]
    core = me & 1
    block = out_ref.shape[1]
    which = pl.program_id(0)
    if mu:
        own = [ref[...] for ref in parts[:2]]
        high = high_of(me, mu)

        @pl.when(which == 0)
        def _():
            out_ref[...] = first_ref[...] - jnp.concatenate(ordered(flip, *own), 0)

        @pl.when(which == 1)
        def _():
            got = [
                jnp.where(high == 1, a[...], b[...])
                for a, b in zip(parts[2:4], parts[4:6])
            ]
            whole = jnp.concatenate(ordered(flip, *got), 0)
            out_ref[...] = first_ref[...] - whole.T
    else:
        half = block // 2
        own = ordered(flip, parts[0][...], parts[1][...])
        got = ordered(flip, parts[2][...], parts[3][...])

        @pl.when(which == 0)
        def _():
            whole = jnp.concatenate([p[:half] for p in own], 0)
            out_ref[...] = first_ref[...] - whole

        @pl.when(which == 1)
        def _():
            mine = jnp.concatenate([p[half:] for p in own], 0)
            theirs = jnp.concatenate([p[half:] for p in got], 0)
            whole = jnp.concatenate(
                [
                    jnp.where(core == 0, mine, theirs),
                    jnp.where(core == 0, theirs, mine),
                ],
                0,
            )
            out_ref[...] = first_ref[...] - jnp.where(core == 0, whole, whole.T)


def finish(info, first_section, previous, parts, mu):
    rows, width = first_section.shape

    def column(k, info):
        me = info[0]
        if mu:
            both = (owned_column(me, mu), received_column(me, mu))
        else:
            both = (me, me ^ 1)
        return 0, jnp.where(k == 0, *both)

    chained = previous is not None
    specs = [pl.BlockSpec((rows, rows), column)]
    operands = [first_section]
    if chained:
        specs.append(pl.BlockSpec(memory_space=ANY))
        operands.append(previous)
    for part in parts:
        specs.append(pl.BlockSpec(part.shape, lambda k, info: (0, 0)))
        operands.append(part)
    return pl.pallas_call(
        functools.partial(finish_kernel, mu, chained),
        out_shape=jax.ShapeDtypeStruct(first_section.shape, F32),
        grid_spec=pltpu.PrefetchScalarGridSpec(
            num_scalar_prefetch=1,
            grid=(2,),
            in_specs=specs,
            out_specs=pl.BlockSpec((rows, rows), column),
        ),
        input_output_aliases={2: 0} if chained else {},
        cost_estimate=pl.CostEstimate(
            flops=rows * rows * 2, bytes_accessed=rows * rows * 32, transcendentals=0
        ),
        name=f"finish_{mu}",
    )(info, *operands)


def triangular_body(inv_factor, border, block_rows, live_count, first_section):
    slots, rows_block, width = border.shape
    devices = lax.axis_size("dev")
    block = width // devices
    bits = list(range(1, devices.bit_length() - 1))
    info = jnp.stack(
        [
            lax.axis_index("dev").astype(jnp.int32),
            (lax.axis_index("grp") & 1).astype(jnp.int32),
            live_count[0],
        ]
    )
    condensed, turned = condense(info, block_rows, inv_factor, border)
    flat = condensed.reshape(slots * rows_block, width)
    waves = list(range(devices // 2 - 1, -1, -1))
    reduced = {}
    for k, mu in enumerate(waves):
        order = tuple(bits if k % 2 == 0 else bits[::-1]) + ("z",)
        kept, sent = products(info, flat, turned, block, mu, order)
        reduced[mu] = reduce_wave(kept, sent, order)
    result = None
    for mu in waves:
        own = reduced[mu]
        if mu:
            direct = [swap(x, "dev", 2 * mu) for x in own]
            parts = (*own, *direct, *[swap(x, "dev", 1) for x in direct])
        else:
            parts = (*own, *[swap(x, "dev", 1) for x in own])
        result = finish(info, first_section, result, parts, mu)
    return condensed, result


def solution(mesh):
    placed = (
        P(("grp", "dev"), None, None),
        P(("grp", "dev"), None, None),
        P(("grp", "dev")),
        P(("grp", "dev")),
        P("dev", None),
    )

    def body(inv_factor, border, block_rows, live_count, first_section):
        rows, width = first_section.shape
        devices, groups = mesh.shape["dev"], mesh.shape["grp"]
        fits = (
            power_of_two(devices)
            and devices >= 4
            and power_of_two(groups)
            and rows % 256 == 0
            and border.shape[1] % 128 == 0
        )
        run = triangular_body if fits else plain_body
        return run(inv_factor, border, block_rows, live_count, first_section)

    return jax.shard_map(
        body,
        mesh=mesh,
        in_specs=placed,
        out_specs=(P(("grp", "dev"), None, None), P("dev", None)),
        check_vma=False,
    )
```

```python
import functools

import jax
import jax.numpy as jnp
from jax import lax
from jax.experimental import pallas as pl
from jax.experimental.pallas import tpu as pltpu
from jax.sharding import PartitionSpec as P


F32 = jnp.float32
ANY = pl.ANY


def power_of_two(n):
    return n >= 2 and n & (n - 1) == 0


def plain_body(inv_factor, border, block_rows, live_count, first_section):
    slots, rows_block, _ = border.shape
    row_ids = lax.broadcasted_iota(jnp.int32, (slots, rows_block, 1), 1)
    slot_ids = lax.broadcasted_iota(jnp.int32, (slots, rows_block, 1), 0)
    keep = (row_ids < block_rows[:, None, None]) & (slot_ids < live_count[0])
    masked = jnp.where(keep, inv_factor, jnp.zeros_like(inv_factor))
    condensed = jnp.einsum(
        "srk,skc->src", masked, border, preferred_element_type=F32
    ).astype(border.dtype)
    flat = condensed.reshape(slots * rows_block, -1)
    partial = lax.dot_general(
        flat, flat, (((0,), (0,)), ((), ())), preferred_element_type=F32
    )
    share = lax.psum_scatter(partial, "dev", scatter_dimension=0, tiled=True)
    return condensed, first_section - lax.psum(share, "grp")


SHARED = "shared"
DIAGONAL = "diagonal"


def heights(block, parts):
    of = {SHARED: block // 4, DIAGONAL: 3 * block // 8}
    return [of.get(part, block // 2) for part in parts]


def dot_turned(left, right):
    return lax.dot_general(
        left, right, (((0,), (0,)), ((), ())), preferred_element_type=F32
    )


def store_piece(wave, refs, info, chip_at, owner_core, half, row, value):
    _, order = wave
    z = half ^ info[1]
    where = []
    for b in order:
        where.append(z if b == "z" else (chip_at >> (b - 1)) & 1)
    sends = owner_core ^ (info[0] & 1)
    for ref, mine in zip(refs, (0, 1)):

        @pl.when(sends == mine)
        def _():
            ref[(*where, pl.ds(row, value.shape[0]), slice(None))] = value


def pair_products(wave, part, refs, info, read, ratio, block):
    chip = info[0] >> 1
    one, two = chip ^ ratio, chip ^ ratio ^ part
    low, high = jnp.minimum(one, two), jnp.maximum(one, two)
    whole = dot_turned(read(low), read(high))
    row = sum(heights(block, wave[0])[: wave[0].index(part)])
    half = block // 2
    for a in range(2):
        for b in range(2):
            at = (low if a == b else high) ^ chip
            for j in range(2):
                top = a * block + j * half
                value = whole[top : top + half, b * block : (b + 1) * block]
                store_piece(wave, refs, info, at, b, j, row, value)


def own_products(waves, refs, info, read, ratio, block):
    at = info[0] >> 1 ^ ratio
    columns = read(at)
    whole = dot_turned(columns, columns)
    half, quarter, eighth = block // 2, block // 4, block // 8
    for wave, pair in zip(waves, refs):
        rows = heights(block, wave[0])
        for part, start in zip(wave[0], [sum(rows[:k]) for k in range(len(rows))]):
            for core in range(2):
                for j in range(2):
                    if part == SHARED:
                        top = core * half + j * quarter
                        value = whole[top : top + quarter, block:]
                        store_piece(wave, pair, info, ratio, core, j, start, value)
                    if part == DIAGONAL:
                        low = core * block
                        top = low + j * quarter
                        value = whole[top : top + quarter, low : low + block]
                        store_piece(wave, pair, info, ratio, core, j, start, value)
                        top = low + half + j * quarter
                        corner = whole[top : top + quarter, low + half : low + block]
                        value = jnp.concatenate([corner[:eighth], corner[eighth:]], 1)
                        store_piece(
                            wave, pair, info, ratio, core, j, start + quarter, value
                        )


def product_steps(waves, chips):
    steps = []
    for wave in waves:
        for part in wave[0]:
            if isinstance(part, int):
                steps += [(part, r) for r in range(chips) if r < r ^ part]
    if any(isinstance(p, str) for w in waves for p in w[0]):
        steps += [(None, r) for r in range(chips)]
    return steps


def run_products(waves, steps, at, refs, info, read, block):
    pairs = [refs[2 * k : 2 * k + 2] for k in range(len(waves))]
    for k, (part, ratio) in enumerate(steps):

        @pl.when(at == k)
        def _():
            if part is None:
                own_products(waves, pairs, info, read, ratio, block)
            else:
                which = [k for k, w in enumerate(waves) if part in w[0]][0]
                pair_products(
                    waves[which], part, pairs[which], info, read, ratio, block
                )


def wave_shapes(waves, block):
    shapes = []
    for parts, order in waves:
        shape = (2,) * len(order) + (sum(heights(block, parts)), block)
        shapes += [jax.ShapeDtypeStruct(shape, F32)] * 2
    return shapes


def whole_block(shape):
    return pl.BlockSpec(shape, lambda *_: (0,) * len(shape))


def condense_kernel(waves, steps, tiles, block, info, rows, *refs):
    inv_ref, border_ref, out_ref, *wave_refs, held = refs
    step = pl.program_id(0)
    filling = steps[0]
    depth, tile = out_ref.shape[1], out_ref.shape[2]
    slot = step // tiles
    live = slot < info[2]

    def put(value):
        out_ref[0] = value
        row = pl.multiple_of(slot * depth, depth)
        column = pl.multiple_of((step % tiles) * tile, tile)
        held[pl.ds(row, depth), pl.ds(column, tile)] = value

    @pl.when((step < filling) & live)
    def _():
        inv = inv_ref[0]
        row_ids = lax.broadcasted_iota(jnp.int32, inv.shape, 0)
        inv = jnp.where(row_ids < rows[slot], inv, jnp.zeros_like(inv))
        product = jnp.dot(inv, border_ref[0], preferred_element_type=F32)
        put(product.astype(out_ref.dtype))

    @pl.when((step < filling) & jnp.logical_not(live))
    def _():
        put(jnp.zeros(out_ref.shape[1:], out_ref.dtype))

    def read(chip):
        return held[:, pl.ds(pl.multiple_of(chip * 2 * block, 2 * block), 2 * block)]

    run_products(waves, steps[1], step - filling, wave_refs, info, read, block)


def condense(info, block_rows, inv_factor, border, waves, devices, tile=1024):
    slots, rows, width = border.shape
    block = width // devices
    tile = min(tile, width)
    tiles = width // tile
    filling = slots * tiles
    products = product_steps(waves, devices // 2)

    def slot_of(step, info):
        return jnp.minimum(step // tiles, info[2] - 1)

    def source(step, info, rows_):
        live = step // tiles < info[2]
        return slot_of(step, info), 0, jnp.where(live, step % tiles, tiles - 1)

    def target(step, info, rows_):
        at = jnp.minimum(step, filling - 1)
        return at // tiles, 0, at % tiles

    shapes = wave_shapes(waves, block)
    return pl.pallas_call(
        functools.partial(condense_kernel, waves, (filling, products), tiles, block),
        out_shape=(jax.ShapeDtypeStruct(border.shape, border.dtype), *shapes),
        grid_spec=pltpu.PrefetchScalarGridSpec(
            num_scalar_prefetch=2,
            grid=(filling + len(products),),
            in_specs=[
                pl.BlockSpec(
                    (1, rows, rows), lambda s, info, rows_: (slot_of(s, info), 0, 0)
                ),
                pl.BlockSpec((1, rows, tile), source),
            ],
            out_specs=(
                pl.BlockSpec((1, rows, tile), target),
                *[whole_block(s.shape) for s in shapes],
            ),
            scratch_shapes=[pltpu.VMEM((slots * rows, width), border.dtype)],
        ),
        compiler_params=pltpu.CompilerParams(vmem_limit_bytes=32 << 20),
        cost_estimate=pl.CostEstimate(
            flops=6 * slots * rows * rows * width,
            bytes_accessed=2 * border.size * 2,
            transcendentals=0,
        ),
        name="condense",
    )(info, block_rows, inv_factor, border)


def products_kernel(waves, steps, block, info, held, *wave_refs):
    def read(chip):
        return held[:, pl.ds(pl.multiple_of(chip * 2 * block, 2 * block), 2 * block)]

    run_products(waves, steps, pl.program_id(0), wave_refs, info, read, block)


def products(info, condensed, waves, devices):
    depth, width = condensed.shape
    block = width // devices
    steps = product_steps(waves, devices // 2)
    shapes = wave_shapes(waves, block)
    return pl.pallas_call(
        functools.partial(products_kernel, waves, steps, block),
        out_shape=tuple(shapes),
        grid_spec=pltpu.PrefetchScalarGridSpec(
            num_scalar_prefetch=1,
            grid=(len(steps),),
            in_specs=[whole_block(condensed.shape)],
            out_specs=tuple(whole_block(s.shape) for s in shapes),
        ),
        compiler_params=pltpu.CompilerParams(vmem_limit_bytes=32 << 20),
        cost_estimate=pl.CostEstimate(
            flops=2 * depth * 4 * block * block * len(steps),
            bytes_accessed=condensed.size * 2,
            transcendentals=0,
        ),
        name="products",
    )(info, condensed)


def swap(x, axis, bits):
    n = lax.axis_size(axis)
    return lax.ppermute(x, axis, [(i, i ^ bits) for i in range(n)])


def after(x, *others):
    return lax.optimization_barrier((x, *others))[0]


def ordered(flip, first, second):
    return jnp.where(flip == 0, first, second), jnp.where(flip == 0, second, first)


def finish_kernel(part, chained, info, first_ref, *refs):
    refs = refs[1:] if chained else refs
    *parts, out_ref = refs
    me, flip = info[0], info[1]
    core = me & 1
    block = out_ref.shape[1]
    which = pl.program_id(0)
    own = ordered(flip, parts[0][...], parts[1][...])
    if part == DIAGONAL:
        half, quarter = block // 2, block // 4
        top = jnp.concatenate([p[:quarter] for p in own], 0)
        corner = [q for p in own for q in (p[quarter:, :half], p[quarter:, half:])]
        low = jnp.concatenate([top[:, half:].T, jnp.concatenate(corner, 0)], 1)
        out_ref[...] = first_ref[...] - jnp.concatenate([top, low], 0)
    elif part == SHARED:
        got = ordered(flip, parts[2][...], parts[3][...])
        own, got = jnp.concatenate(own, 0), jnp.concatenate(got, 0)
        whole = jnp.concatenate(
            [jnp.where(core == 0, own, got), jnp.where(core == 0, got, own)], 0
        )
        out_ref[...] = first_ref[...] - jnp.where(core == 0, whole, whole.T)
    else:
        chip = me >> 1
        high = (chip ^ part) < chip

        def put(halves):
            whole = jnp.concatenate(halves, 0)
            out_ref[...] = first_ref[...] - jnp.where(high, whole.T, whole)

        @pl.when(which == 0)
        def _():
            put(own)

        @pl.when(which == 1)
        def _():
            got = [
                jnp.where(high, a[...], b[...])
                for a, b in zip(parts[2:4], parts[4:6])
            ]
            put(ordered(flip, *got))


def finish(info, first_section, previous, parts, part):
    rows, _ = first_section.shape

    def column(k, info):
        me = info[0]
        if part == DIAGONAL:
            return 0, me
        if part == SHARED:
            return 0, me ^ 1
        chip = me >> 1
        high = ((chip ^ part) < chip).astype(jnp.int32)
        return 0, me ^ (2 * part) ^ (k ^ high)

    chained = previous is not None
    specs = [pl.BlockSpec((rows, rows), column)]
    operands = [first_section]
    if chained:
        specs.append(pl.BlockSpec(memory_space=ANY))
        operands.append(previous)
    for one in parts:
        specs.append(whole_block(one.shape))
        operands.append(one)
    return pl.pallas_call(
        functools.partial(finish_kernel, part, chained),
        out_shape=jax.ShapeDtypeStruct(first_section.shape, F32),
        grid_spec=pltpu.PrefetchScalarGridSpec(
            num_scalar_prefetch=1,
            grid=(1 if isinstance(part, str) else 2,),
            in_specs=specs,
            out_specs=pl.BlockSpec((rows, rows), column),
        ),
        input_output_aliases={2: 0} if chained else {},
        compiler_params=pltpu.CompilerParams(vmem_limit_bytes=16 << 20),
        cost_estimate=pl.CostEstimate(
            flops=rows * rows * 2, bytes_accessed=rows * rows * 32, transcendentals=0
        ),
    )(info, *operands)


def split(x, rows):
    out, at = [], 0
    for n in rows:
        out.append(x[at : at + n])
        at += n
    return out


def plan(devices):
    chips = devices // 2
    bits = list(range(1, devices.bit_length() - 1))
    axes = [*bits, "z"]
    contents = [(mu,) for mu in range(chips - 1, 0, -1)]
    turns = [k % len(axes) for k in range(len(contents))]
    waves = [(c, (*axes[k:], *axes[:k])) for c, k in zip(contents, turns)]
    waves.append(((SHARED, DIAGONAL), (bits[0], "z", *bits[1:])))
    return waves


def triangular_body(inv_factor, border, block_rows, live_count, first_section):
    slots, rows_block, width = border.shape
    devices = lax.axis_size("dev")
    groups = lax.axis_size("grp")
    block = width // devices
    info = jnp.stack(
        [
            lax.axis_index("dev").astype(jnp.int32),
            (lax.axis_index("grp") & 1).astype(jnp.int32),
            live_count[0],
        ]
    )
    waves = plan(devices)
    early, late = waves[:2], waves[2:]
    condensed, *arrays = condense(
        info, block_rows, inv_factor, border, early, devices
    )
    flat = condensed.reshape(slots * rows_block, width)

    def first_step(pair):
        kept, sent = pair
        got = swap(sent, "dev", 1)
        return kept[0] + got[0], kept[1] + got[1]

    state = [first_step(arrays[2 * k : 2 * k + 2]) for k in range(len(early))]
    arrays = products(after(info, *[s[1] for s in state]), flat, late, devices)
    state += [first_step(arrays[2 * k : 2 * k + 2]) for k in range(len(late))]

    def finish_reduction(wave, kept, send):
        parts, order = wave
        for k, step in enumerate(order):
            where = ("grp", 1) if step == "z" else ("dev", 1 << step)
            got = swap(send, *where)
            if k + 1 < len(order):
                kept, send = kept[0] + got[0], kept[1] + got[1]
        mine = kept + got
        bit = 2
        while bit < groups:
            got = swap(mine, "grp", bit)
            bit *= 2
            if bit < groups:
                mine = mine + got
        rows = heights(block, parts)
        own = [a + b for a, b in zip(split(mine, rows), split(got, rows))]
        return {p: (x, swap(x, "grp", 1)) for p, x in zip(parts, own)}

    reduced = {}
    for wave, pair in zip(waves, state):
        reduced.update(finish_reduction(wave, *pair))
    result = None
    *pairs, last = [p for parts, _ in waves[:-1] for p in parts]
    for part in (*pairs, SHARED, DIAGONAL, last):
        pieces = reduced[part]
        if part == SHARED:
            pieces = (*pieces, *[swap(x, "dev", 1) for x in pieces])
        elif part != DIAGONAL:
            direct = [swap(x, "dev", 2 * part) for x in pieces]
            pieces = (*pieces, *direct, *[swap(x, "dev", 1) for x in direct])
        result = finish(info, first_section, result, pieces, part)
    return condensed, result


def solution(mesh):
    placed = (
        P(("grp", "dev"), None, None),
        P(("grp", "dev"), None, None),
        P(("grp", "dev")),
        P(("grp", "dev")),
        P("dev", None),
    )

    def body(inv_factor, border, block_rows, live_count, first_section):
        rows, _ = first_section.shape
        devices, groups = mesh.shape["dev"], mesh.shape["grp"]
        fits = (
            power_of_two(devices)
            and devices >= 4
            and power_of_two(groups)
            and groups >= 4
            and rows % 256 == 0
            and border.shape[1] % 128 == 0
        )
        run = triangular_body if fits else plain_body
        return run(inv_factor, border, block_rows, live_count, first_section)

    return jax.shard_map(
        body,
        mesh=mesh,
        in_specs=placed,
        out_specs=(P(("grp", "dev"), None, None), P("dev", None)),
        check_vma=False,
    )
```
